1024 devices in a mesh: ta: 64 (over z, x), xyz: 16 (over y, core).
Axes of the slice: x: 4, y: 8, z: 16, core: 2. Of those that a mesh axis runs over, the one named last changes fastest.
Arguments:
- right_side: bfloat16 [64, 16, 2, 2, 128], P('ta', 'xyz'), may hold values from -24 to 24
- self_block: bfloat16 [64, 16, 2, 2, 64, 128], P('ta', 'xyz'), may hold values from -1 to 4
- hop_blocks: bfloat16 [64, 16, 2, 2, 4, 64, 128], P('ta', 'xyz'), may hold values from -0.125 to 0.125
Outputs:
- solution: float32 [64, 16, 2, 2, 128], P('ta', 'xyz')
- final_residual: float32 [64, 16, 2, 2, 128], P('ta', 'xyz')
The draws below stay inside these ranges and needn't reach their ends.
All inputs are finite; a program needn't handle non-finite values.
Results may differ from the reference program's by a relative error of at most 0.011.
Values may be sent and summed in bfloat16 or wider, within the bound.
No kernel may reach another device: no remote copies, remote signals or barrier semaphores. Data moves between devices by JAX's collectives and lax.ppermute only.
A program may use at most 32 MiB of HBM per device.

```python
import math
import jax
import jax.numpy as jnp
from jax import lax

NC = 64
NR = 128
LX = 2
LY = 2
ITERS = 3
LT = 64
LZ = 16


def draw_right_side(key, part):
    noise_key, rough_key = jax.random.split(key)
    full_shape = (LT, LZ, LY, LX, NR)
    time_axis = jnp.arange(LT, dtype=jnp.float32).reshape(LT, 1, 1, 1, 1)
    rough_factor = jax.random.uniform(rough_key, (LT, LZ, LY, LX, 1), minval=0.5, maxval=1.5)
    time_ramp = 1.0 + 2.0 * time_axis / (LT - 1)
    noise_part = jnp.clip(jax.random.normal(noise_key, full_shape), -4.0, 4.0)
    return (noise_part * rough_factor * time_ramp).astype(jnp.bfloat16)


def draw_self_block(key, part):
    noise_key, diag_key = jax.random.split(key)
    full_shape = (LT, LZ, LY, LX, NC, NR)
    spread_scale = 0.3 / math.sqrt(NC)
    noise_part = jnp.clip(jax.random.normal(noise_key, full_shape), -4.0, 4.0) * spread_scale
    diagonal = jax.random.uniform(diag_key, (LT, LZ, LY, LX, NC, 1), minval=1.5, maxval=3.0)
    on_diagonal = (jnp.arange(NR)[None, :] == jnp.arange(NC)[:, None]).astype(jnp.float32)
    return (noise_part + diagonal * on_diagonal).astype(jnp.bfloat16)


def steps_of(key, dims, cuts, smallest, largest):
    def one(position, parts):
        draws = jax.random.uniform(jax.random.fold_in(jax.random.fold_in(key, 6), position), (parts,), jnp.float32, smallest / len(cuts), largest / len(cuts))
        return jnp.repeat(jnp.exp(draws), dims[position] // parts).reshape((-1,) + (1,) * (len(dims) - position - 1))

    gain = one(*cuts[0])
    for cut in cuts[1:]:
        gain = gain * one(*cut)
    return gain


def scatter_about(key, dims, scale, bound, cuts=(), held_as=jnp.bfloat16):
    values = scale * jax.random.normal(key, dims, jnp.float32)
    if cuts:
        values = values * steps_of(key, dims, cuts, -0.22, 0.18)
    return jnp.clip(values, -bound, bound).astype(held_as)


def setup_inputs(seed: int = 0) -> dict:
    key_list = jax.random.split(jax.random.key(seed), 4)
    right_side = draw_right_side(jax.random.fold_in(key_list[3], 71), 0)
    self_block = draw_self_block(jax.random.fold_in(key_list[3], 71), 0)
    hop_blocks = scatter_about(key_list[2], (LT, LZ, LY, LX, 4, NC, NR), (32 * NC) ** -0.5, 0.125, ((0, 64), (1, 16)))
    return {"right_side": right_side, "self_block": self_block, "hop_blocks": hop_blocks}


def chirality_signs(full_width):
    half_width = full_width // 2
    quarter = full_width // 4
    column = jnp.arange(full_width) % half_width
    return jnp.where(column < quarter, 1.0, -1.0).astype(jnp.float32)

def forward_apply(blocks, vector):
    half_width = blocks.shape[-2]
    real_in = vector[..., :half_width]
    imag_in = vector[..., half_width:]
    plain_order = jnp.concatenate([real_in, -imag_in], -1).astype(jnp.float32)
    turned = jnp.concatenate([imag_in, real_in], -1).astype(jnp.float32)
    matrix = blocks.astype(jnp.float32)
    real_out = jnp.einsum('...ab,...b->...a', matrix, plain_order, precision=lax.Precision.HIGHEST)
    imag_out = jnp.einsum('...ab,...b->...a', matrix, turned, precision=lax.Precision.HIGHEST)
    return jnp.concatenate([real_out, imag_out], -1)

def adjoint_apply(blocks, vector):
    half_width = blocks.shape[-2]
    matrix = blocks.astype(jnp.float32)
    from_real = jnp.einsum('...ab,...a->...b', matrix, vector[..., :half_width].astype(jnp.float32), precision=lax.Precision.HIGHEST)
    from_imag = jnp.einsum('...ab,...a->...b', matrix, vector[..., half_width:].astype(jnp.float32), precision=lax.Precision.HIGHEST)
    return jnp.concatenate([from_real[..., :half_width] + from_imag[..., half_width:], from_imag[..., :half_width] - from_real[..., half_width:]], -1)

def apply_operator(vector_field, self_block, hop_blocks):
    rounded = vector_field.astype(jnp.bfloat16)
    chiral_signs = chirality_signs(vector_field.shape[-1])
    flipped = rounded * chiral_signs.astype(jnp.bfloat16)
    summed = forward_apply(self_block, rounded)
    for hop_index, roll_axis in enumerate((3, 2, 1, 0)):
        blocks = hop_blocks[..., hop_index, :, :]
        summed = summed + forward_apply(blocks, jnp.roll(rounded, -1, roll_axis))
        carried = adjoint_apply(blocks, flipped).astype(jnp.bfloat16)
        summed = summed + chiral_signs * jnp.roll(carried, 1, roll_axis).astype(jnp.float32)
    return summed

def inner_pair(left_vec, right_vec):
    half_width = left_vec.shape[-1] // 2
    real_part = jnp.sum(left_vec[..., :half_width] * right_vec[..., :half_width] + left_vec[..., half_width:] * right_vec[..., half_width:])
    imag_part = jnp.sum(left_vec[..., :half_width] * right_vec[..., half_width:] - left_vec[..., half_width:] * right_vec[..., :half_width])
    return (real_part, imag_part)

def scale_complex(real_part, imag_part, vector):
    half_width = vector.shape[-1] // 2
    vec_re = vector[..., :half_width]
    vec_im = vector[..., half_width:]
    return jnp.concatenate([real_part * vec_re - imag_part * vec_im, real_part * vec_im + imag_part * vec_re], -1)

def reference(right_side, self_block, hop_blocks):
    residual = right_side.astype(jnp.float32)
    solution = jnp.zeros_like(residual)
    basis_list = []
    direction_list = []
    for iteration in range(ITERS):
        mapped = apply_operator(residual, self_block, hop_blocks)
        projections = [inner_pair(basis_vec, mapped) for basis_vec in basis_list]
        squared = inner_pair(mapped, mapped)[0]
        along_re, along_im = inner_pair(mapped, residual)
        orthogonal = mapped
        direction = residual
        for (proj_re, proj_im), basis_vec, previous in zip(projections, basis_list, direction_list):
            squared = squared - (proj_re * proj_re + proj_im * proj_im)
            orthogonal = orthogonal - scale_complex(proj_re, proj_im, basis_vec)
            direction = direction - scale_complex(proj_re, proj_im, previous)
        length = jnp.sqrt(squared)
        new_basis = orthogonal / length
        new_direction = direction / length
        step_re = along_re / length
        step_im = along_im / length
        solution = solution + scale_complex(step_re, step_im, new_direction)
        residual = residual - scale_complex(step_re, step_im, new_basis)
        basis_list.append(new_basis)
        direction_list.append(new_direction)
    return (solution, residual)
```

```python
import jax
import jax.numpy as jnp
from jax import lax
from jax.experimental import pallas as pl
from jax.experimental.pallas import tpu as pltpu
from jax.sharding import Mesh
from jax.sharding import PartitionSpec as P

ITERS = 3
T_AXES = ("tz", "tx")
Z_AXES = ("sy", "sc")
DIAGONAL = (1, 2, 3)
PAIRS = ((0, 1), (0, 2), (0, 3), (1, 2), (1, 3), (2, 3))


def shifted(block, axes, distance):
    count = lax.axis_size(axes)
    route = [((i - distance) % count, i) for i in range(count)]
    return lax.ppermute(block, axes, route)


def chirality_signs(full_width):
    half_width = full_width // 2
    column = jnp.arange(full_width) % half_width
    return jnp.where(column < half_width // 2, 1.0, -1.0).astype(jnp.float32)


def forward_sum(blocks, vectors):
    half = blocks.shape[-2]
    plain = jnp.concatenate([vectors[..., :half], -vectors[..., half:]], -1)
    turned = jnp.concatenate([vectors[..., half:], vectors[..., :half]], -1)
    wide = blocks.astype(jnp.float32)
    real_out = jnp.sum(wide * plain[..., None, :], (-3, -1))
    imag_out = jnp.sum(wide * turned[..., None, :], (-3, -1))
    return jnp.concatenate([real_out, imag_out], -1)


def adjoint(blocks, vector):
    half = blocks.shape[-2]
    wide = blocks.astype(jnp.float32)
    from_real = jnp.sum(wide * vector[..., None, :half, None], -2)
    from_imag = jnp.sum(wide * vector[..., None, half:, None], -2)
    return jnp.concatenate(
        [
            from_real[..., :half] + from_imag[..., half:],
            from_imag[..., :half] - from_real[..., half:],
        ],
        -1,
    )


def apply_operator(field, self_block, hop_blocks):
    signs = chirality_signs(field.shape[-1])
    ahead_z = shifted(field, Z_AXES, -1)
    ahead_t = shifted(field, T_AXES, -1)
    carried = adjoint(hop_blocks, field * signs)
    behind_z = shifted(carried[:, :, 2], Z_AXES, 1)
    behind_t = shifted(carried[:, :, 3], T_AXES, 1)
    near = forward_sum(self_block[:, :, None], field[:, :, None])
    near_hops = jnp.stack([jnp.roll(field, -1, 1), jnp.roll(field, -1, 0)], 2)
    near = near + forward_sum(hop_blocks[:, :, :2], near_hops)
    near_back = jnp.roll(carried[:, :, 0], 1, 1) + jnp.roll(carried[:, :, 1], 1, 0)
    far = forward_sum(hop_blocks[:, :, 2:], jnp.stack([ahead_z, ahead_t], 2))
    return near + far + signs * (near_back + behind_z + behind_t)


def gram_body(v0, v1, v2, v3, out):
    vectors = [v0[...], v1[...], v2[...], v3[...]]
    half = vectors[0].shape[-1] // 2
    lane = lax.broadcasted_iota(jnp.int32, vectors[0].shape, 1)
    sign = jnp.where(lane < half, 1.0, -1.0)
    turned = [pltpu.roll(v, half, 1) * sign for v in vectors]
    rows = [jnp.sum(vectors[i] * vectors[i], 0, keepdims=True) for i in DIAGONAL]
    for i, j in PAIRS:
        rows.append(jnp.sum(vectors[i] * vectors[j], 0, keepdims=True))
        rows.append(jnp.sum(vectors[i] * turned[j], 0, keepdims=True))
    rows.append(jnp.zeros_like(rows[0]))
    stacked = jnp.concatenate(rows, 0)
    totals = jnp.sum(stacked, 1, keepdims=True)
    row = lax.broadcasted_iota(jnp.int32, stacked.shape, 0)
    column = lax.broadcasted_iota(jnp.int32, stacked.shape, 1)
    out[...] = jnp.sum(jnp.where(row == column, totals, 0.0), 0, keepdims=True)


def cmul(a, b):
    return (a[0] * b[0] - a[1] * b[1], a[0] * b[1] + a[1] * b[0])


def cmulc(a, b):
    return (a[0] * b[0] + a[1] * b[1], a[0] * b[1] - a[1] * b[0])


def cadd(a, b):
    return (a[0] + b[0], a[1] + b[1])


def csub(a, b):
    return (a[0] - b[0], a[1] - b[1])


def gram_image(gram, vec):
    image = {}
    for i in range(4):
        total = None
        for j, value in vec.items():
            if (i, j) not in gram:
                continue
            term = cmul(gram[i, j], value)
            total = term if total is None else cadd(total, term)
        image[i] = total
    return image


def inner(left, image):
    total = None
    for i, value in left.items():
        term = cmulc(value, image[i])
        total = term if total is None else cadd(total, term)
    return total


def combine(base, scale, vec):
    out = dict(base)
    for i, value in vec.items():
        term = cmul(scale, value)
        out[i] = csub(out[i], term) if i in out else (-term[0], -term[1])
    return out


def cycle_coefficients(gram, one):
    zero = jnp.zeros_like(one)
    residual = {0: (one, zero)}
    answer = {}
    basis_list = []
    direction_list = []
    for _ in range(ITERS):
        mapped = {i + 1: value for i, value in residual.items()}
        image = gram_image(gram, mapped)
        norm = inner(mapped, image)[0]
        along = inner(residual, image)
        along = (along[0], -along[1])
        orthogonal = mapped
        direction = residual
        squared = norm
        for basis, previous in zip(basis_list, direction_list):
            proj = inner(basis, image)
            squared = squared - (proj[0] * proj[0] + proj[1] * proj[1])
            orthogonal = combine(orthogonal, proj, basis)
            direction = combine(direction, proj, previous)
        scale = 1.0 / jnp.sqrt(squared)
        new_basis = {i: (v[0] * scale, v[1] * scale) for i, v in orthogonal.items()}
        new_direction = {i: (v[0] * scale, v[1] * scale) for i, v in direction.items()}
        step = (along[0] * scale, along[1] * scale)
        minus = (-step[0], -step[1])
        answer = combine(answer, minus, new_direction)
        residual = combine(residual, step, new_basis)
        basis_list.append(new_basis)
        direction_list.append(new_direction)
    return answer, residual


def gram_of(totals):
    gram = {}
    for k, i in enumerate(DIAGONAL):
        gram[i, i] = (totals[k], jnp.zeros_like(totals[k]))
    for k, (i, j) in enumerate(PAIRS):
        real, imag = totals[3 + 2 * k], totals[4 + 2 * k]
        gram[i, j] = (real, imag)
        gram[j, i] = (real, -imag)
    return gram


def finish_body(packed, v0, v1, v2, v3, answer_out, residual_out):
    vectors = [v0[...], v1[...], v2[...], v3[...]]
    half = vectors[0].shape[-1] // 2
    spread = jnp.broadcast_to(packed[...], (16, 2 * half))
    row = lax.broadcasted_iota(jnp.int32, spread.shape, 0)
    column = lax.broadcasted_iota(jnp.int32, spread.shape, 1)
    totals = jnp.sum(jnp.where(row == column, spread, 0.0), 1, keepdims=True)
    entries = [totals[k : k + 1, :] for k in range(15)]
    answer, residual = cycle_coefficients(gram_of(entries), jnp.ones_like(entries[0]))
    lane = lax.broadcasted_iota(jnp.int32, vectors[0].shape, 1)
    sign = jnp.where(lane < half, -1.0, 1.0)
    turned = [pltpu.roll(v, half, 1) * sign for v in vectors]
    for coefficients, out in ((answer, answer_out), (residual, residual_out)):
        total = None
        for i, (real, imag) in coefficients.items():
            term = real * vectors[i] + imag * turned[i]
            total = term if total is None else total + term
        out[...] = total


def whole_sum(packed):
    for axes in (("sy", "sc"), "tx", "tz"):
        packed = lax.psum(packed, axes)
    return packed


def on_device(right_side, self_block, hop_blocks):
    shape = right_side.shape
    sites = shape[2:]
    rows = (sites[0] * sites[1], sites[2])
    local_self = self_block[0, 0]
    local_hops = hop_blocks[0, 0]
    vectors = [right_side[0, 0].astype(jnp.float32)]
    for _ in range(ITERS):
        vectors.append(apply_operator(vectors[-1], local_self, local_hops))
    flat = [v.reshape(rows) for v in vectors]
    space = pl.BlockSpec(memory_space=pltpu.VMEM)
    packed = pl.pallas_call(
        gram_body,
        out_shape=jax.ShapeDtypeStruct((1, rows[1]), jnp.float32),
        in_specs=[space] * 4,
        out_specs=space,
    )(*flat)
    packed = whole_sum(packed)
    result = jax.ShapeDtypeStruct(rows, jnp.float32)
    answer, residual = pl.pallas_call(
        finish_body,
        out_shape=(result, result),
        in_specs=[space] * 5,
        out_specs=(space, space),
    )(packed, *flat)
    return answer.reshape(shape), residual.reshape(shape)


def solution(mesh):
    chips = mesh.devices.reshape(16, 4, 8, 2)
    fine = Mesh(chips, (*T_AXES, *Z_AXES))
    lead = (T_AXES, Z_AXES)
    placed = (P(*lead), P(*lead), P(*lead))
    return jax.shard_map(
        on_device,
        mesh=fine,
        in_specs=placed,
        out_specs=(P(*lead), P(*lead)),
        check_vma=False,
    )
```

```python
import jax
import jax.numpy as jnp
from jax import lax
from jax.experimental import pallas as pl
from jax.experimental.pallas import tpu as pltpu
from jax.sharding import Mesh
from jax.sharding import PartitionSpec as P

ITERS = 3
T_AXES = ("tz", "tx")
Z_AXES = ("sy", "sc")
DIAGONAL = (1, 2, 3)
PAIRS = ((0, 1), (0, 2), (0, 3), (1, 2), (1, 3), (2, 3))


def shifted(block, axes, distance):
    count = lax.axis_size(axes)
    route = [((i - distance) % count, i) for i in range(count)]
    return lax.ppermute(block, axes, route)


def chirality_signs(full_width):
    half_width = full_width // 2
    column = jnp.arange(full_width) % half_width
    return jnp.where(column < half_width // 2, 1.0, -1.0).astype(jnp.float32)


def forward_sum(blocks, vectors):
    half = blocks.shape[-2]
    plain = jnp.concatenate([vectors[..., :half], -vectors[..., half:]], -1)
    turned = jnp.concatenate([vectors[..., half:], vectors[..., :half]], -1)
    wide = blocks.astype(jnp.float32)
    real_out = jnp.sum(wide * plain[..., None, :], (-3, -1))
    imag_out = jnp.sum(wide * turned[..., None, :], (-3, -1))
    return jnp.concatenate([real_out, imag_out], -1)


def adjoint(blocks, vector):
    half = blocks.shape[-2]
    wide = blocks.astype(jnp.float32)
    from_real = jnp.sum(wide * vector[..., None, :half, None], -2)
    from_imag = jnp.sum(wide * vector[..., None, half:, None], -2)
    return jnp.concatenate(
        [
            from_real[..., :half] + from_imag[..., half:],
            from_imag[..., :half] - from_real[..., half:],
        ],
        -1,
    )


def apply_operator(field, self_block, hop_blocks):
    signs = chirality_signs(field.shape[-1])
    ahead_z = shifted(field, Z_AXES, -1)
    ahead_t = shifted(field, T_AXES, -1)
    carried = adjoint(hop_blocks, field * signs)
    behind_z = shifted(carried[:, :, 2], Z_AXES, 1)
    behind_t = shifted(carried[:, :, 3], T_AXES, 1)
    near = forward_sum(self_block[:, :, None], field[:, :, None])
    near_hops = jnp.stack([jnp.roll(field, -1, 1), jnp.roll(field, -1, 0)], 2)
    near = near + forward_sum(hop_blocks[:, :, :2], near_hops)
    near_back = jnp.roll(carried[:, :, 0], 1, 1) + jnp.roll(carried[:, :, 1], 1, 0)
    far = forward_sum(hop_blocks[:, :, 2:], jnp.stack([ahead_z, ahead_t], 2))
    return near + far + signs * (near_back + behind_z + behind_t)


def gram_body(v0, v1, v2, v3, out):
    vectors = [v0[...], v1[...], v2[...], v3[...]]
    half = vectors[0].shape[-1] // 2
    lane = lax.broadcasted_iota(jnp.int32, vectors[0].shape, 1)
    sign = jnp.where(lane < half, 1.0, -1.0)
    turned = [pltpu.roll(v, half, 1) * sign for v in vectors]
    rows = [jnp.sum(vectors[i] * vectors[i], 0, keepdims=True) for i in DIAGONAL]
    for i, j in PAIRS:
        rows.append(jnp.sum(vectors[i] * vectors[j], 0, keepdims=True))
        rows.append(jnp.sum(vectors[i] * turned[j], 0, keepdims=True))
    rows.append(jnp.zeros_like(rows[0]))
    stacked = jnp.concatenate(rows, 0)
    totals = jnp.sum(stacked, 1, keepdims=True)
    row = lax.broadcasted_iota(jnp.int32, stacked.shape, 0)
    column = lax.broadcasted_iota(jnp.int32, stacked.shape, 1)
    out[...] = jnp.sum(jnp.where(row == column, totals, 0.0), 0, keepdims=True)


def cmul(a, b):
    return (a[0] * b[0] - a[1] * b[1], a[0] * b[1] + a[1] * b[0])


def cmulc(a, b):
    return (a[0] * b[0] + a[1] * b[1], a[0] * b[1] - a[1] * b[0])


def cadd(a, b):
    return (a[0] + b[0], a[1] + b[1])


def csub(a, b):
    return (a[0] - b[0], a[1] - b[1])


def gram_image(gram, vec):
    image = {}
    for i in range(4):
        total = None
        for j, value in vec.items():
            if (i, j) not in gram:
                continue
            term = cmul(gram[i, j], value)
            total = term if total is None else cadd(total, term)
        image[i] = total
    return image


def inner(left, image):
    total = None
    for i, value in left.items():
        term = cmulc(value, image[i])
        total = term if total is None else cadd(total, term)
    return total


def combine(base, scale, vec):
    out = dict(base)
    for i, value in vec.items():
        term = cmul(scale, value)
        out[i] = csub(out[i], term) if i in out else (-term[0], -term[1])
    return out


def cycle_coefficients(gram, one):
    zero = jnp.zeros_like(one)
    residual = {0: (one, zero)}
    answer = {}
    basis_list = []
    direction_list = []
    for _ in range(ITERS):
        mapped = {i + 1: value for i, value in residual.items()}
        image = gram_image(gram, mapped)
        norm = inner(mapped, image)[0]
        along = inner(residual, image)
        along = (along[0], -along[1])
        orthogonal = mapped
        direction = residual
        squared = norm
        for basis, previous in zip(basis_list, direction_list):
            proj = inner(basis, image)
            squared = squared - (proj[0] * proj[0] + proj[1] * proj[1])
            orthogonal = combine(orthogonal, proj, basis)
            direction = combine(direction, proj, previous)
        scale = 1.0 / jnp.sqrt(squared)
        new_basis = {i: (v[0] * scale, v[1] * scale) for i, v in orthogonal.items()}
        new_direction = {i: (v[0] * scale, v[1] * scale) for i, v in direction.items()}
        step = (along[0] * scale, along[1] * scale)
        minus = (-step[0], -step[1])
        answer = combine(answer, minus, new_direction)
        residual = combine(residual, step, new_basis)
        basis_list.append(new_basis)
        direction_list.append(new_direction)
    return answer, residual


def gram_of(totals):
    gram = {}
    for k, i in enumerate(DIAGONAL):
        gram[i, i] = (totals[k], jnp.zeros_like(totals[k]))
    for k, (i, j) in enumerate(PAIRS):
        real, imag = totals[3 + 2 * k], totals[4 + 2 * k]
        gram[i, j] = (real, imag)
        gram[j, i] = (real, -imag)
    return gram


def finish_body(packed, v0, v1, v2, v3, answer_out, residual_out):
    vectors = [v0[...], v1[...], v2[...], v3[...]]
    half = vectors[0].shape[-1] // 2
    spread = jnp.broadcast_to(packed[...], (16, 2 * half))
    row = lax.broadcasted_iota(jnp.int32, spread.shape, 0)
    column = lax.broadcasted_iota(jnp.int32, spread.shape, 1)
    totals = jnp.sum(jnp.where(row == column, spread, 0.0), 1, keepdims=True)
    entries = [totals[k : k + 1, :] for k in range(15)]
    answer, residual = cycle_coefficients(gram_of(entries), jnp.ones_like(entries[0]))
    lane = lax.broadcasted_iota(jnp.int32, vectors[0].shape, 1)
    sign = jnp.where(lane < half, -1.0, 1.0)
    turned = [pltpu.roll(v, half, 1) * sign for v in vectors]
    for coefficients, out in ((answer, answer_out), (residual, residual_out)):
        total = None
        for i, (real, imag) in coefficients.items():
            term = real * vectors[i] + imag * turned[i]
            total = term if total is None else total + term
        out[...] = total


def whole_sum(packed):
    for axes in (("sy", "sc"), "tx", "tz"):
        count = lax.axis_size(axes)
        copies = jnp.broadcast_to(packed, (count, packed.shape[1]))
        got = lax.all_to_all(copies, axes, 0, 0, tiled=True)
        packed = jnp.sum(got, 0, keepdims=True)
    return packed


def on_device(right_side, self_block, hop_blocks):
    shape = right_side.shape
    sites = shape[2:]
    rows = (sites[0] * sites[1], sites[2])
    local_self = self_block[0, 0]
    local_hops = hop_blocks[0, 0]
    vectors = [right_side[0, 0].astype(jnp.float32)]
    for _ in range(ITERS):
        vectors.append(apply_operator(vectors[-1], local_self, local_hops))
    flat = [v.reshape(rows) for v in vectors]
    space = pl.BlockSpec(memory_space=pltpu.VMEM)
    packed = pl.pallas_call(
        gram_body,
        out_shape=jax.ShapeDtypeStruct((1, rows[1]), jnp.float32),
        in_specs=[space] * 4,
        out_specs=space,
    )(*flat)
    packed = whole_sum(packed)
    result = jax.ShapeDtypeStruct(rows, jnp.float32)
    answer, residual = pl.pallas_call(
        finish_body,
        out_shape=(result, result),
        in_specs=[space] * 5,
        out_specs=(space, space),
    )(packed, *flat)
    return answer.reshape(shape), residual.reshape(shape)


def solution(mesh):
    chips = mesh.devices.reshape(16, 4, 8, 2)
    fine = Mesh(chips, (*T_AXES, *Z_AXES))
    lead = (T_AXES, Z_AXES)
    placed = (P(*lead), P(*lead), P(*lead))
    return jax.shard_map(
        on_device,
        mesh=fine,
        in_specs=placed,
        out_specs=(P(*lead), P(*lead)),
        check_vma=False,
    )
```

```python
import jax
import jax.numpy as jnp
from jax import lax
from jax.experimental import pallas as pl
from jax.experimental.pallas import tpu as pltpu
from jax.sharding import Mesh
from jax.sharding import PartitionSpec as P

ITERS = 3
T_AXES = ("tz", "tx")
Z_AXES = ("sy", "sc")
DIAGONAL = (1, 2, 3)
PAIRS = ((0, 1), (0, 2), (0, 3), (1, 2), (1, 3), (2, 3))


def exchanged(field, carried, axes):
    count = lax.axis_size(axes)
    even = lax.axis_index(axes) % 2 == 0
    inside = lax.ppermute(
        jnp.where(even, carried, field), axes, [(i, i ^ 1) for i in range(count)]
    )
    across = lax.ppermute(
        jnp.where(even, field, carried),
        axes,
        [(i, (i + (1 if i % 2 else -1)) % count) for i in range(count)],
    )
    return jnp.where(even, inside, across), jnp.where(even, across, inside)


def chirality_signs(full_width):
    half_width = full_width // 2
    column = jnp.arange(full_width) % half_width
    return jnp.where(column < half_width // 2, 1.0, -1.0).astype(jnp.float32)


def forward_sum(blocks, vectors):
    half = blocks.shape[-2]
    plain = jnp.concatenate([vectors[..., :half], -vectors[..., half:]], -1)
    turned = jnp.concatenate([vectors[..., half:], vectors[..., :half]], -1)
    wide = blocks.astype(jnp.float32)
    real_out = jnp.sum(wide * plain[..., None, :], (-3, -1))
    imag_out = jnp.sum(wide * turned[..., None, :], (-3, -1))
    return jnp.concatenate([real_out, imag_out], -1)


def adjoint(blocks, vector):
    half = blocks.shape[-2]
    wide = blocks.astype(jnp.float32)
    from_real = jnp.sum(wide * vector[..., None, :half, None], -2)
    from_imag = jnp.sum(wide * vector[..., None, half:, None], -2)
    return jnp.concatenate(
        [
            from_real[..., :half] + from_imag[..., half:],
            from_imag[..., :half] - from_real[..., half:],
        ],
        -1,
    )


def apply_operator(field, self_block, hop_blocks):
    signs = chirality_signs(field.shape[-1])
    carried = adjoint(hop_blocks, field * signs)
    ahead_t, behind_t = exchanged(field, carried[:, :, 3], T_AXES)
    ahead_z, behind_z = exchanged(field, carried[:, :, 2], Z_AXES)
    near = forward_sum(self_block[:, :, None], field[:, :, None])
    near_hops = jnp.stack([jnp.roll(field, -1, 1), jnp.roll(field, -1, 0)], 2)
    near = near + forward_sum(hop_blocks[:, :, :2], near_hops)
    near_back = jnp.roll(carried[:, :, 0], 1, 1) + jnp.roll(carried[:, :, 1], 1, 0)
    far = forward_sum(hop_blocks[:, :, 2:], jnp.stack([ahead_z, ahead_t], 2))
    return near + far + signs * (near_back + behind_z + behind_t)


def gram_body(v0, v1, v2, v3, out):
    vectors = [v0[...], v1[...], v2[...], v3[...]]
    half = vectors[0].shape[-1] // 2
    lane = lax.broadcasted_iota(jnp.int32, vectors[0].shape, 1)
    sign = jnp.where(lane < half, 1.0, -1.0)
    turned = [pltpu.roll(v, half, 1) * sign for v in vectors]
    rows = [jnp.sum(vectors[i] * vectors[i], 0, keepdims=True) for i in DIAGONAL]
    for i, j in PAIRS:
        rows.append(jnp.sum(vectors[i] * vectors[j], 0, keepdims=True))
        rows.append(jnp.sum(vectors[i] * turned[j], 0, keepdims=True))
    rows.append(jnp.zeros_like(rows[0]))
    stacked = jnp.concatenate(rows, 0)
    totals = jnp.sum(stacked, 1, keepdims=True)
    row = lax.broadcasted_iota(jnp.int32, stacked.shape, 0)
    column = lax.broadcasted_iota(jnp.int32, stacked.shape, 1)
    out[...] = jnp.sum(jnp.where(row == column, totals, 0.0), 0, keepdims=True)


def cmul(a, b):
    return (a[0] * b[0] - a[1] * b[1], a[0] * b[1] + a[1] * b[0])


def cmulc(a, b):
    return (a[0] * b[0] + a[1] * b[1], a[0] * b[1] - a[1] * b[0])


def cadd(a, b):
    return (a[0] + b[0], a[1] + b[1])


def csub(a, b):
    return (a[0] - b[0], a[1] - b[1])


def gram_image(gram, vec):
    image = {}
    for i in range(4):
        total = None
        for j, value in vec.items():
            if (i, j) not in gram:
                continue
            term = cmul(gram[i, j], value)
            total = term if total is None else cadd(total, term)
        image[i] = total
    return image


def inner(left, image):
    total = None
    for i, value in left.items():
        term = cmulc(value, image[i])
        total = term if total is None else cadd(total, term)
    return total


def combine(base, scale, vec):
    out = dict(base)
    for i, value in vec.items():
        term = cmul(scale, value)
        out[i] = csub(out[i], term) if i in out else (-term[0], -term[1])
    return out


def cycle_coefficients(gram, one):
    zero = jnp.zeros_like(one)
    residual = {0: (one, zero)}
    answer = {}
    basis_list = []
    direction_list = []
    for _ in range(ITERS):
        mapped = {i + 1: value for i, value in residual.items()}
        image = gram_image(gram, mapped)
        norm = inner(mapped, image)[0]
        along = inner(residual, image)
        along = (along[0], -along[1])
        orthogonal = mapped
        direction = residual
        squared = norm
        for basis, previous in zip(basis_list, direction_list):
            proj = inner(basis, image)
            squared = squared - (proj[0] * proj[0] + proj[1] * proj[1])
            orthogonal = combine(orthogonal, proj, basis)
            direction = combine(direction, proj, previous)
        scale = 1.0 / jnp.sqrt(squared)
        new_basis = {i: (v[0] * scale, v[1] * scale) for i, v in orthogonal.items()}
        new_direction = {i: (v[0] * scale, v[1] * scale) for i, v in direction.items()}
        step = (along[0] * scale, along[1] * scale)
        minus = (-step[0], -step[1])
        answer = combine(answer, minus, new_direction)
        residual = combine(residual, step, new_basis)
        basis_list.append(new_basis)
        direction_list.append(new_direction)
    return answer, residual


def gram_of(totals):
    gram = {}
    for k, i in enumerate(DIAGONAL):
        gram[i, i] = (totals[k], jnp.zeros_like(totals[k]))
    for k, (i, j) in enumerate(PAIRS):
        real, imag = totals[3 + 2 * k], totals[4 + 2 * k]
        gram[i, j] = (real, imag)
        gram[j, i] = (real, -imag)
    return gram


def finish_body(packed, v0, v1, v2, v3, answer_out, residual_out):
    vectors = [v0[...], v1[...], v2[...], v3[...]]
    half = vectors[0].shape[-1] // 2
    spread = jnp.broadcast_to(packed[...], (16, 2 * half))
    row = lax.broadcasted_iota(jnp.int32, spread.shape, 0)
    column = lax.broadcasted_iota(jnp.int32, spread.shape, 1)
    totals = jnp.sum(jnp.where(row == column, spread, 0.0), 1, keepdims=True)
    entries = [totals[k : k + 1, :] for k in range(15)]
    answer, residual = cycle_coefficients(gram_of(entries), jnp.ones_like(entries[0]))
    lane = lax.broadcasted_iota(jnp.int32, vectors[0].shape, 1)
    sign = jnp.where(lane < half, -1.0, 1.0)
    turned = [pltpu.roll(v, half, 1) * sign for v in vectors]
    for coefficients, out in ((answer, answer_out), (residual, residual_out)):
        total = None
        for i, (real, imag) in coefficients.items():
            term = real * vectors[i] + imag * turned[i]
            total = term if total is None else total + term
        out[...] = total


def whole_sum(packed):
    for axes in (("tx", "sy", "sc"), "tz"):
        count = lax.axis_size(axes)
        copies = jnp.broadcast_to(packed, (count, packed.shape[1]))
        got = lax.all_to_all(copies, axes, 0, 0, tiled=True)
        packed = jnp.sum(got, 0, keepdims=True)
    return packed


def on_device(right_side, self_block, hop_blocks):
    shape = right_side.shape
    sites = shape[2:]
    rows = (sites[0] * sites[1], sites[2])
    local_self = self_block[0, 0]
    local_hops = hop_blocks[0, 0]
    vectors = [right_side[0, 0].astype(jnp.float32)]
    for _ in range(ITERS):
        vectors.append(apply_operator(vectors[-1], local_self, local_hops))
    flat = [v.reshape(rows) for v in vectors]
    space = pl.BlockSpec(memory_space=pltpu.VMEM)
    packed = pl.pallas_call(
        gram_body,
        out_shape=jax.ShapeDtypeStruct((1, rows[1]), jnp.float32),
        in_specs=[space] * 4,
        out_specs=space,
    )(*flat)
    packed = whole_sum(packed)
    result = jax.ShapeDtypeStruct(rows, jnp.float32)
    answer, residual = pl.pallas_call(
        finish_body,
        out_shape=(result, result),
        in_specs=[space] * 5,
        out_specs=(space, space),
    )(packed, *flat)
    return answer.reshape(shape), residual.reshape(shape)


def solution(mesh):
    chips = mesh.devices.reshape(16, 4, 8, 2)
    fine = Mesh(chips, (*T_AXES, *Z_AXES))
    lead = (T_AXES, Z_AXES)
    placed = (P(*lead), P(*lead), P(*lead))
    return jax.shard_map(
        on_device,
        mesh=fine,
        in_specs=placed,
        out_specs=(P(*lead), P(*lead)),
        check_vma=False,
    )
```

```python
import jax
import jax.numpy as jnp
from jax import lax
from jax.experimental import pallas as pl
from jax.experimental.pallas import tpu as pltpu
from jax.sharding import Mesh
from jax.sharding import PartitionSpec as P

ITERS = 3
T_AXES = ("tz", "tx")
Z_AXES = ("sy", "sc")
DIAGONAL = (1, 2, 3)
PAIRS = ((0, 1), (0, 2), (0, 3), (1, 2), (1, 3), (2, 3))


def shifted(block, axes, distance):
    count = lax.axis_size(axes)
    route = [((i - distance) % count, i) for i in range(count)]
    return lax.ppermute(block, axes, route)


def chirality_signs(full_width):
    half_width = full_width // 2
    column = jnp.arange(full_width) % half_width
    return jnp.where(column < half_width // 2, 1.0, -1.0).astype(jnp.float32)


def forward_sum(blocks, vectors):
    half = blocks.shape[-2]
    plain = jnp.concatenate([vectors[..., :half], -vectors[..., half:]], -1)
    turned = jnp.concatenate([vectors[..., half:], vectors[..., :half]], -1)
    wide = blocks.astype(jnp.float32)
    real_out = jnp.sum(wide * plain[..., None, :], (-3, -1))
    imag_out = jnp.sum(wide * turned[..., None, :], (-3, -1))
    return jnp.concatenate([real_out, imag_out], -1)


def adjoint(blocks, vector):
    half = blocks.shape[-2]
    wide = blocks.astype(jnp.float32)
    from_real = jnp.sum(wide * vector[..., None, :half, None], -2)
    from_imag = jnp.sum(wide * vector[..., None, half:, None], -2)
    return jnp.concatenate(
        [
            from_real[..., :half] + from_imag[..., half:],
            from_imag[..., :half] - from_real[..., half:],
        ],
        -1,
    )


def apply_operator(field, self_block, hop_blocks):
    signs = chirality_signs(field.shape[-1])
    ahead_z = shifted(field, Z_AXES, -1)
    ahead_t = shifted(field, T_AXES, -1)
    carried = adjoint(hop_blocks, field * signs)
    behind_z = shifted(carried[:, :, 2], Z_AXES, 1)
    behind_t = shifted(carried[:, :, 3], T_AXES, 1)
    near = forward_sum(self_block[:, :, None], field[:, :, None])
    near_hops = jnp.stack([jnp.roll(field, -1, 1), jnp.roll(field, -1, 0)], 2)
    near = near + forward_sum(hop_blocks[:, :, :2], near_hops)
    near_back = jnp.roll(carried[:, :, 0], 1, 1) + jnp.roll(carried[:, :, 1], 1, 0)
    far = forward_sum(hop_blocks[:, :, 2:], jnp.stack([ahead_z, ahead_t], 2))
    return near + far + signs * (near_back + behind_z + behind_t)


def gram_body(v0, v1, v2, v3, out):
    vectors = [v0[...], v1[...], v2[...], v3[...]]
    half = vectors[0].shape[-1] // 2
    lane = lax.broadcasted_iota(jnp.int32, vectors[0].shape, 1)
    sign = jnp.where(lane < half, 1.0, -1.0)
    turned = [pltpu.roll(v, half, 1) * sign for v in vectors]
    rows = [jnp.sum(vectors[i] * vectors[i], 0, keepdims=True) for i in DIAGONAL]
    for i, j in PAIRS:
        rows.append(jnp.sum(vectors[i] * vectors[j], 0, keepdims=True))
        rows.append(jnp.sum(vectors[i] * turned[j], 0, keepdims=True))
    rows.append(jnp.zeros_like(rows[0]))
    stacked = jnp.concatenate(rows, 0)
    totals = jnp.sum(stacked, 1, keepdims=True)
    row = lax.broadcasted_iota(jnp.int32, stacked.shape, 0)
    column = lax.broadcasted_iota(jnp.int32, stacked.shape, 1)
    out[...] = jnp.sum(jnp.where(row == column, totals, 0.0), 0, keepdims=True)


def cmul(a, b):
    return (a[0] * b[0] - a[1] * b[1], a[0] * b[1] + a[1] * b[0])


def cmulc(a, b):
    return (a[0] * b[0] + a[1] * b[1], a[0] * b[1] - a[1] * b[0])


def cadd(a, b):
    return (a[0] + b[0], a[1] + b[1])


def csub(a, b):
    return (a[0] - b[0], a[1] - b[1])


def gram_image(gram, vec):
    image = {}
    for i in range(4):
        total = None
        for j, value in vec.items():
            if (i, j) not in gram:
                continue
            term = cmul(gram[i, j], value)
            total = term if total is None else cadd(total, term)
        image[i] = total
    return image


def inner(left, image):
    total = None
    for i, value in left.items():
        term = cmulc(value, image[i])
        total = term if total is None else cadd(total, term)
    return total


def combine(base, scale, vec):
    out = dict(base)
    for i, value in vec.items():
        term = cmul(scale, value)
        out[i] = csub(out[i], term) if i in out else (-term[0], -term[1])
    return out


def cycle_coefficients(gram, one):
    zero = jnp.zeros_like(one)
    residual = {0: (one, zero)}
    answer = {}
    basis_list = []
    direction_list = []
    for _ in range(ITERS):
        mapped = {i + 1: value for i, value in residual.items()}
        image = gram_image(gram, mapped)
        norm = inner(mapped, image)[0]
        along = inner(residual, image)
        along = (along[0], -along[1])
        orthogonal = mapped
        direction = residual
        squared = norm
        for basis, previous in zip(basis_list, direction_list):
            proj = inner(basis, image)
            squared = squared - (proj[0] * proj[0] + proj[1] * proj[1])
            orthogonal = combine(orthogonal, proj, basis)
            direction = combine(direction, proj, previous)
        scale = 1.0 / jnp.sqrt(squared)
        new_basis = {i: (v[0] * scale, v[1] * scale) for i, v in orthogonal.items()}
        new_direction = {i: (v[0] * scale, v[1] * scale) for i, v in direction.items()}
        step = (along[0] * scale, along[1] * scale)
        minus = (-step[0], -step[1])
        answer = combine(answer, minus, new_direction)
        residual = combine(residual, step, new_basis)
        basis_list.append(new_basis)
        direction_list.append(new_direction)
    return answer, residual


def gram_of(totals):
    gram = {}
    for k, i in enumerate(DIAGONAL):
        gram[i, i] = (totals[k], jnp.zeros_like(totals[k]))
    for k, (i, j) in enumerate(PAIRS):
        real, imag = totals[3 + 2 * k], totals[4 + 2 * k]
        gram[i, j] = (real, imag)
        gram[j, i] = (real, -imag)
    return gram


def finish_body(packed, v0, v1, v2, v3, answer_out, residual_out):
    vectors = [v0[...], v1[...], v2[...], v3[...]]
    half = vectors[0].shape[-1] // 2
    spread = jnp.broadcast_to(packed[...], (16, 2 * half))
    row = lax.broadcasted_iota(jnp.int32, spread.shape, 0)
    column = lax.broadcasted_iota(jnp.int32, spread.shape, 1)
    totals = jnp.sum(jnp.where(row == column, spread, 0.0), 1, keepdims=True)
    entries = [totals[k : k + 1, :] for k in range(15)]
    answer, residual = cycle_coefficients(gram_of(entries), jnp.ones_like(entries[0]))
    lane = lax.broadcasted_iota(jnp.int32, vectors[0].shape, 1)
    sign = jnp.where(lane < half, -1.0, 1.0)
    turned = [pltpu.roll(v, half, 1) * sign for v in vectors]
    for coefficients, out in ((answer, answer_out), (residual, residual_out)):
        total = None
        for i, (real, imag) in coefficients.items():
            term = real * vectors[i] + imag * turned[i]
            total = term if total is None else total + term
        out[...] = total


def whole_sum(packed):
    for axes in (("tx", "sy", "sc"), "tz"):
        count = lax.axis_size(axes)
        copies = jnp.broadcast_to(packed, (count, packed.shape[1]))
        got = lax.all_to_all(copies, axes, 0, 0, tiled=True)
        packed = jnp.sum(got, 0, keepdims=True)
    return packed


def on_device(right_side, self_block, hop_blocks):
    shape = right_side.shape
    sites = shape[2:]
    rows = (sites[0] * sites[1], sites[2])
    local_self = self_block[0, 0]
    local_hops = hop_blocks[0, 0]
    vectors = [right_side[0, 0].astype(jnp.float32)]
    for _ in range(ITERS):
        vectors.append(apply_operator(vectors[-1], local_self, local_hops))
    flat = [v.reshape(rows) for v in vectors]
    space = pl.BlockSpec(memory_space=pltpu.VMEM)
    packed = pl.pallas_call(
        gram_body,
        out_shape=jax.ShapeDtypeStruct((1, rows[1]), jnp.float32),
        in_specs=[space] * 4,
        out_specs=space,
    )(*flat)
    packed = whole_sum(packed)
    result = jax.ShapeDtypeStruct(rows, jnp.float32)
    answer, residual = pl.pallas_call(
        finish_body,
        out_shape=(result, result),
        in_specs=[space] * 5,
        out_specs=(space, space),
    )(packed, *flat)
    return answer.reshape(shape), residual.reshape(shape)


def solution(mesh):
    chips = mesh.devices.reshape(16, 4, 8, 2)
    fine = Mesh(chips, (*T_AXES, *Z_AXES))
    lead = (T_AXES, Z_AXES)
    placed = (P(*lead), P(*lead), P(*lead))
    return jax.shard_map(
        on_device,
        mesh=fine,
        in_specs=placed,
        out_specs=(P(*lead), P(*lead)),
        check_vma=False,
    )
```

```python
import jax
import jax.numpy as jnp
from jax import lax
from jax.experimental import pallas as pl
from jax.experimental.pallas import tpu as pltpu
from jax.sharding import Mesh
from jax.sharding import PartitionSpec as P


ITERS = 3
T_AXES = ("tz", "tx")
Z_AXES = ("sy", "sc")
DIAGONAL = (1, 2, 3)
PAIRS = ((0, 1), (0, 2), (0, 3), (1, 2), (1, 3), (2, 3))


def shifted(block, axes, distance):
    count = lax.axis_size(axes)
    route = [((i - distance) % count, i) for i in range(count)]
    return lax.ppermute(block, axes, route)


def chirality_signs(full_width):
    half_width = full_width // 2
    column = jnp.arange(full_width) % half_width
    return jnp.where(column < half_width // 2, 1.0, -1.0).astype(jnp.float32)


def forward_sum(blocks, vectors):
    half = blocks.shape[-2]
    plain = jnp.concatenate([vectors[..., :half], -vectors[..., half:]], -1)
    turned = jnp.concatenate([vectors[..., half:], vectors[..., :half]], -1)
    wide = blocks.astype(jnp.float32)
    real_out = jnp.sum(wide * plain[..., None, :], (-3, -1))
    imag_out = jnp.sum(wide * turned[..., None, :], (-3, -1))
    return jnp.concatenate([real_out, imag_out], -1)


def adjoint(blocks, vector):
    half = blocks.shape[-2]
    wide = blocks.astype(jnp.float32)
    from_real = jnp.sum(wide * vector[..., None, :half, None], -2)
    from_imag = jnp.sum(wide * vector[..., None, half:, None], -2)
    return jnp.concatenate(
        [
            from_real[..., :half] + from_imag[..., half:],
            from_imag[..., :half] - from_real[..., half:],
        ],
        -1,
    )


def apply_operator(field, self_block, hop_blocks):
    signs = chirality_signs(field.shape[-1])
    ahead_t = shifted(field, T_AXES, -1)
    ahead_z = shifted(field, Z_AXES, -1)
    carried = adjoint(hop_blocks, field * signs)
    behind_t = shifted(carried[:, :, 3], T_AXES, 1)
    behind_z = shifted(carried[:, :, 2], Z_AXES, 1)
    near = forward_sum(self_block[:, :, None], field[:, :, None])
    near_hops = jnp.stack([jnp.roll(field, -1, 1), jnp.roll(field, -1, 0)], 2)
    near = near + forward_sum(hop_blocks[:, :, :2], near_hops)
    near_back = jnp.roll(carried[:, :, 0], 1, 1) + jnp.roll(carried[:, :, 1], 1, 0)
    far = forward_sum(hop_blocks[:, :, 2:], jnp.stack([ahead_z, ahead_t], 2))
    return near + far + signs * (near_back + behind_z + behind_t)


def gram_body(v0, v1, v2, v3, out):
    vectors = [v0[...], v1[...], v2[...], v3[...]]
    half = vectors[0].shape[-1] // 2
    lane = lax.broadcasted_iota(jnp.int32, vectors[0].shape, 1)
    sign = jnp.where(lane < half, 1.0, -1.0)
    turned = [pltpu.roll(v, half, 1) * sign for v in vectors]
    rows = [jnp.sum(vectors[i] * vectors[i], 0, keepdims=True) for i in DIAGONAL]
    for i, j in PAIRS:
        rows.append(jnp.sum(vectors[i] * vectors[j], 0, keepdims=True))
        rows.append(jnp.sum(vectors[i] * turned[j], 0, keepdims=True))
    rows.append(jnp.zeros_like(rows[0]))
    stacked = jnp.concatenate(rows, 0)
    totals = jnp.sum(stacked, 1, keepdims=True)
    row = lax.broadcasted_iota(jnp.int32, stacked.shape, 0)
    column = lax.broadcasted_iota(jnp.int32, stacked.shape, 1)
    packed = jnp.sum(jnp.where(row == column, totals, 0.0), 0, keepdims=True)
    out[...] = jnp.broadcast_to(packed[None], out.shape)


def cmul(a, b):
    return (a[0] * b[0] - a[1] * b[1], a[0] * b[1] + a[1] * b[0])


def cmulc(a, b):
    return (a[0] * b[0] + a[1] * b[1], a[0] * b[1] - a[1] * b[0])


def cadd(a, b):
    return (a[0] + b[0], a[1] + b[1])


def csub(a, b):
    return (a[0] - b[0], a[1] - b[1])


def gram_image(gram, vec):
    image = {}
    for i in range(4):
        total = None
        for j, value in vec.items():
            if (i, j) not in gram:
                continue
            term = cmul(gram[i, j], value)
            total = term if total is None else cadd(total, term)
        image[i] = total
    return image


def inner(left, image):
    total = None
    for i, value in left.items():
        term = cmulc(value, image[i])
        total = term if total is None else cadd(total, term)
    return total


def combine(base, scale, vec):
    out = dict(base)
    for i, value in vec.items():
        term = cmul(scale, value)
        out[i] = csub(out[i], term) if i in out else (-term[0], -term[1])
    return out


def cycle_coefficients(gram, one):
    zero = jnp.zeros_like(one)
    residual = {0: (one, zero)}
    answer = {}
    basis_list = []
    direction_list = []
    for _ in range(ITERS):
        mapped = {i + 1: value for i, value in residual.items()}
        image = gram_image(gram, mapped)
        norm = inner(mapped, image)[0]
        along = inner(residual, image)
        along = (along[0], -along[1])
        orthogonal = mapped
        direction = residual
        squared = norm
        for basis, previous in zip(basis_list, direction_list):
            proj = inner(basis, image)
            squared = squared - (proj[0] * proj[0] + proj[1] * proj[1])
            orthogonal = combine(orthogonal, proj, basis)
            direction = combine(direction, proj, previous)
        scale = 1.0 / jnp.sqrt(squared)
        new_basis = {i: (v[0] * scale, v[1] * scale) for i, v in orthogonal.items()}
        new_direction = {i: (v[0] * scale, v[1] * scale) for i, v in direction.items()}
        step = (along[0] * scale, along[1] * scale)
        minus = (-step[0], -step[1])
        answer = combine(answer, minus, new_direction)
        residual = combine(residual, step, new_basis)
        basis_list.append(new_basis)
        direction_list.append(new_direction)
    return answer, residual


def gram_of(totals):
    gram = {}
    for k, i in enumerate(DIAGONAL):
        gram[i, i] = (totals[k], jnp.zeros_like(totals[k]))
    for k, (i, j) in enumerate(PAIRS):
        real, imag = totals[3 + 2 * k], totals[4 + 2 * k]
        gram[i, j] = (real, imag)
        gram[j, i] = (real, -imag)
    return gram


def finish_body(gathered, v0, v1, v2, v3, answer_out, residual_out):
    vectors = [v0[...], v1[...], v2[...], v3[...]]
    half = vectors[0].shape[-1] // 2
    spread = jnp.broadcast_to(jnp.sum(gathered[...], 0), (16, 2 * half))
    row = lax.broadcasted_iota(jnp.int32, spread.shape, 0)
    column = lax.broadcasted_iota(jnp.int32, spread.shape, 1)
    totals = jnp.sum(jnp.where(row == column, spread, 0.0), 1, keepdims=True)
    entries = [totals[k : k + 1, :] for k in range(15)]
    answer, residual = cycle_coefficients(gram_of(entries), jnp.ones_like(entries[0]))
    lane = lax.broadcasted_iota(jnp.int32, vectors[0].shape, 1)
    sign = jnp.where(lane < half, -1.0, 1.0)
    turned = [pltpu.roll(v, half, 1) * sign for v in vectors]
    for coefficients, out in ((answer, answer_out), (residual, residual_out)):
        total = None
        for i, (real, imag) in coefficients.items():
            term = real * vectors[i] + imag * turned[i]
            total = term if total is None else total + term
        out[...] = total


def on_chip(array):
    return pltpu.with_memory_space_constraint(array, pltpu.VMEM)


def on_device(right_side, self_block, hop_blocks):
    shape = right_side.shape
    sites = shape[2:]
    rows = (sites[0] * sites[1], sites[2])
    local_self = self_block[0, 0]
    local_hops = hop_blocks[0, 0]
    vectors = [right_side[0, 0].astype(jnp.float32)]
    for _ in range(ITERS):
        vectors.append(apply_operator(vectors[-1], local_self, local_hops))
    flat = [on_chip(v.reshape(rows)) for v in vectors]
    space = pl.BlockSpec(memory_space=pltpu.VMEM)
    near_axes, far_axes = ("tx", "sy", "sc"), "tz"
    copies = pl.pallas_call(
        gram_body,
        out_shape=pltpu.VMEM((lax.axis_size(near_axes), 1, rows[1]), jnp.float32),
        in_specs=[space] * 4,
        out_specs=space,
    )(*flat)
    gathered = lax.all_to_all(copies, near_axes, 0, 0, tiled=True)
    packed = jnp.sum(gathered, 0, keepdims=True)
    copies = jnp.broadcast_to(packed, (lax.axis_size(far_axes), 1, rows[1]))
    gathered = lax.all_to_all(copies, far_axes, 0, 0, tiled=True)
    result = jax.ShapeDtypeStruct(rows, jnp.float32)
    answer, residual = pl.pallas_call(
        finish_body,
        out_shape=(result, result),
        in_specs=[space] * 5,
        out_specs=(space, space),
    )(on_chip(gathered), *flat)
    return answer.reshape(shape), residual.reshape(shape)


def solution(mesh):
    chips = mesh.devices.reshape(16, 4, 8, 2)
    fine = Mesh(chips, (*T_AXES, *Z_AXES))
    lead = (T_AXES, Z_AXES)
    placed = (P(*lead), P(*lead), P(*lead))
    return jax.shard_map(
        on_device,
        mesh=fine,
        in_specs=placed,
        out_specs=(P(*lead), P(*lead)),
        check_vma=False,
    )
```

```python
import jax
import jax.numpy as jnp
from jax import lax
from jax.experimental import pallas as pl
from jax.experimental.pallas import tpu as pltpu
from jax.sharding import Mesh
from jax.sharding import PartitionSpec as P


ITERS = 3
T_AXES = ("tz", "tx")
Z_AXES = ("sy", "sc")
DIAGONAL = (1, 2, 3)
PAIRS = ((0, 1), (0, 2), (0, 3), (1, 2), (1, 3), (2, 3))


def shifted(block, axes, distance):
    count = lax.axis_size(axes)
    route = [((i - distance) % count, i) for i in range(count)]
    return lax.ppermute(block, axes, route)


def exchanged(field, carried, axes):
    count = lax.axis_size(axes)
    even = lax.axis_index(axes) % 2 == 0
    across = lax.ppermute(
        jnp.where(even, field, carried),
        axes,
        [(i, (i + (1 if i % 2 else -1)) % count) for i in range(count)],
    )
    inside = lax.ppermute(
        jnp.where(even, carried, field), axes, [(i, i ^ 1) for i in range(count)]
    )
    return jnp.where(even, inside, across), jnp.where(even, across, inside)


def chirality_signs(full_width):
    half_width = full_width // 2
    column = jnp.arange(full_width) % half_width
    return jnp.where(column < half_width // 2, 1.0, -1.0).astype(jnp.float32)


def forward_sum(blocks, vectors):
    half = blocks.shape[-2]
    plain = jnp.concatenate([vectors[..., :half], -vectors[..., half:]], -1)
    turned = jnp.concatenate([vectors[..., half:], vectors[..., :half]], -1)
    wide = blocks.astype(jnp.float32)
    real_out = jnp.sum(wide * plain[..., None, :], (-3, -1))
    imag_out = jnp.sum(wide * turned[..., None, :], (-3, -1))
    return jnp.concatenate([real_out, imag_out], -1)


def adjoint(blocks, vector):
    half = blocks.shape[-2]
    wide = blocks.astype(jnp.float32)
    from_real = jnp.sum(wide * vector[..., None, :half, None], -2)
    from_imag = jnp.sum(wide * vector[..., None, half:, None], -2)
    return jnp.concatenate(
        [
            from_real[..., :half] + from_imag[..., half:],
            from_imag[..., :half] - from_real[..., half:],
        ],
        -1,
    )


def apply_operator(field, self_block, hop_blocks):
    signs = chirality_signs(field.shape[-1])
    carried = adjoint(hop_blocks, field * signs)
    ahead_t, behind_t = exchanged(field, carried[:, :, 3], T_AXES)
    ahead_z = shifted(field, Z_AXES, -1)
    behind_z = shifted(carried[:, :, 2], Z_AXES, 1)
    near = forward_sum(self_block[:, :, None], field[:, :, None])
    near_hops = jnp.stack([jnp.roll(field, -1, 1), jnp.roll(field, -1, 0)], 2)
    near = near + forward_sum(hop_blocks[:, :, :2], near_hops)
    near_back = jnp.roll(carried[:, :, 0], 1, 1) + jnp.roll(carried[:, :, 1], 1, 0)
    far = forward_sum(hop_blocks[:, :, 2:], jnp.stack([ahead_z, ahead_t], 2))
    return near + far + signs * (near_back + behind_z + behind_t)


def gram_body(v0, v1, v2, v3, out):
    vectors = [v0[...], v1[...], v2[...], v3[...]]
    half = vectors[0].shape[-1] // 2
    lane = lax.broadcasted_iota(jnp.int32, vectors[0].shape, 1)
    sign = jnp.where(lane < half, 1.0, -1.0)
    turned = [pltpu.roll(v, half, 1) * sign for v in vectors]
    rows = [jnp.sum(vectors[i] * vectors[i], 0, keepdims=True) for i in DIAGONAL]
    for i, j in PAIRS:
        rows.append(jnp.sum(vectors[i] * vectors[j], 0, keepdims=True))
        rows.append(jnp.sum(vectors[i] * turned[j], 0, keepdims=True))
    rows.append(jnp.zeros_like(rows[0]))
    stacked = jnp.concatenate(rows, 0)
    totals = jnp.sum(stacked, 1, keepdims=True)
    row = lax.broadcasted_iota(jnp.int32, stacked.shape, 0)
    column = lax.broadcasted_iota(jnp.int32, stacked.shape, 1)
    packed = jnp.sum(jnp.where(row == column, totals, 0.0), 0, keepdims=True)
    out[...] = jnp.broadcast_to(packed[None], out.shape)


def cmul(a, b):
    return (a[0] * b[0] - a[1] * b[1], a[0] * b[1] + a[1] * b[0])


def cmulc(a, b):
    return (a[0] * b[0] + a[1] * b[1], a[0] * b[1] - a[1] * b[0])


def cadd(a, b):
    return (a[0] + b[0], a[1] + b[1])


def csub(a, b):
    return (a[0] - b[0], a[1] - b[1])


def gram_image(gram, vec):
    image = {}
    for i in range(4):
        total = None
        for j, value in vec.items():
            if (i, j) not in gram:
                continue
            term = cmul(gram[i, j], value)
            total = term if total is None else cadd(total, term)
        image[i] = total
    return image


def inner(left, image):
    total = None
    for i, value in left.items():
        term = cmulc(value, image[i])
        total = term if total is None else cadd(total, term)
    return total


def combine(base, scale, vec):
    out = dict(base)
    for i, value in vec.items():
        term = cmul(scale, value)
        out[i] = csub(out[i], term) if i in out else (-term[0], -term[1])
    return out


def cycle_coefficients(gram, one):
    zero = jnp.zeros_like(one)
    residual = {0: (one, zero)}
    answer = {}
    basis_list = []
    direction_list = []
    for _ in range(ITERS):
        mapped = {i + 1: value for i, value in residual.items()}
        image = gram_image(gram, mapped)
        norm = inner(mapped, image)[0]
        along = inner(residual, image)
        along = (along[0], -along[1])
        orthogonal = mapped
        direction = residual
        squared = norm
        for basis, previous in zip(basis_list, direction_list):
            proj = inner(basis, image)
            squared = squared - (proj[0] * proj[0] + proj[1] * proj[1])
            orthogonal = combine(orthogonal, proj, basis)
            direction = combine(direction, proj, previous)
        scale = 1.0 / jnp.sqrt(squared)
        new_basis = {i: (v[0] * scale, v[1] * scale) for i, v in orthogonal.items()}
        new_direction = {i: (v[0] * scale, v[1] * scale) for i, v in direction.items()}
        step = (along[0] * scale, along[1] * scale)
        minus = (-step[0], -step[1])
        answer = combine(answer, minus, new_direction)
        residual = combine(residual, step, new_basis)
        basis_list.append(new_basis)
        direction_list.append(new_direction)
    return answer, residual


def gram_of(totals):
    gram = {}
    for k, i in enumerate(DIAGONAL):
        gram[i, i] = (totals[k], jnp.zeros_like(totals[k]))
    for k, (i, j) in enumerate(PAIRS):
        real, imag = totals[3 + 2 * k], totals[4 + 2 * k]
        gram[i, j] = (real, imag)
        gram[j, i] = (real, -imag)
    return gram


def finish_body(gathered, v0, v1, v2, v3, answer_out, residual_out):
    vectors = [v0[...], v1[...], v2[...], v3[...]]
    half = vectors[0].shape[-1] // 2
    spread = jnp.broadcast_to(jnp.sum(gathered[...], 0), (16, 2 * half))
    row = lax.broadcasted_iota(jnp.int32, spread.shape, 0)
    column = lax.broadcasted_iota(jnp.int32, spread.shape, 1)
    totals = jnp.sum(jnp.where(row == column, spread, 0.0), 1, keepdims=True)
    entries = [totals[k : k + 1, :] for k in range(15)]
    answer, residual = cycle_coefficients(gram_of(entries), jnp.ones_like(entries[0]))
    lane = lax.broadcasted_iota(jnp.int32, vectors[0].shape, 1)
    sign = jnp.where(lane < half, -1.0, 1.0)
    turned = [pltpu.roll(v, half, 1) * sign for v in vectors]
    for coefficients, out in ((answer, answer_out), (residual, residual_out)):
        total = None
        for i, (real, imag) in coefficients.items():
            term = real * vectors[i] + imag * turned[i]
            total = term if total is None else total + term
        out[...] = total


def on_chip(array):
    return pltpu.with_memory_space_constraint(array, pltpu.VMEM)


def on_device(right_side, self_block, hop_blocks):
    shape = right_side.shape
    sites = shape[2:]
    rows = (sites[0] * sites[1], sites[2])
    local_self = self_block[0, 0]
    local_hops = hop_blocks[0, 0]
    vectors = [right_side[0, 0].astype(jnp.float32)]
    for _ in range(ITERS):
        vectors.append(apply_operator(vectors[-1], local_self, local_hops))
    flat = [on_chip(v.reshape(rows)) for v in vectors]
    space = pl.BlockSpec(memory_space=pltpu.VMEM)
    near_axes, far_axes = ("tx", "sy", "sc"), "tz"
    copies = pl.pallas_call(
        gram_body,
        out_shape=pltpu.VMEM((lax.axis_size(near_axes), 1, rows[1]), jnp.float32),
        in_specs=[space] * 4,
        out_specs=space,
    )(*flat)
    gathered = lax.all_to_all(copies, near_axes, 0, 0, tiled=True)
    packed = jnp.sum(gathered, 0, keepdims=True)
    copies = jnp.broadcast_to(packed, (lax.axis_size(far_axes), 1, rows[1]))
    gathered = lax.all_to_all(copies, far_axes, 0, 0, tiled=True)
    result = jax.ShapeDtypeStruct(rows, jnp.float32)
    answer, residual = pl.pallas_call(
        finish_body,
        out_shape=(result, result),
        in_specs=[space] * 5,
        out_specs=(space, space),
    )(on_chip(gathered), *flat)
    return answer.reshape(shape), residual.reshape(shape)


def solution(mesh):
    chips = mesh.devices.reshape(16, 4, 8, 2)
    fine = Mesh(chips, (*T_AXES, *Z_AXES))
    lead = (T_AXES, Z_AXES)
    placed = (P(*lead), P(*lead), P(*lead))
    return jax.shard_map(
        on_device,
        mesh=fine,
        in_specs=placed,
        out_specs=(P(*lead), P(*lead)),
        check_vma=False,
    )
```

```python
import jax
import jax.numpy as jnp
from jax import lax
from jax.experimental import pallas as pl
from jax.experimental.pallas import tpu as pltpu
from jax.sharding import Mesh
from jax.sharding import PartitionSpec as P


ITERS = 3
T_AXES = ("tz", "tx")
Z_AXES = ("sy", "sc")
DIAGONAL = (1, 2, 3)
PAIRS = ((0, 1), (0, 2), (0, 3), (1, 2), (1, 3), (2, 3))


def shifted(block, axes, distance):
    count = lax.axis_size(axes)
    route = [((i - distance) % count, i) for i in range(count)]
    return lax.ppermute(block, axes, route)


def exchanged(field, carried, axes):
    count = lax.axis_size(axes)
    even = lax.axis_index(axes) % 2 == 0
    across = lax.ppermute(
        jnp.where(even, field, carried),
        axes,
        [(i, (i + (1 if i % 2 else -1)) % count) for i in range(count)],
    )
    inside = lax.ppermute(
        jnp.where(even, carried, field), axes, [(i, i ^ 1) for i in range(count)]
    )
    return jnp.where(even, inside, across), jnp.where(even, across, inside)


def chirality_signs(full_width):
    half_width = full_width // 2
    column = jnp.arange(full_width) % half_width
    return jnp.where(column < half_width // 2, 1.0, -1.0).astype(jnp.float32)


def forward_sum(blocks, vectors):
    half = blocks.shape[-2]
    plain = jnp.concatenate([vectors[..., :half], -vectors[..., half:]], -1)
    turned = jnp.concatenate([vectors[..., half:], vectors[..., :half]], -1)
    wide = blocks.astype(jnp.float32)
    real_out = jnp.sum(wide * plain[..., None, :], (-3, -1))
    imag_out = jnp.sum(wide * turned[..., None, :], (-3, -1))
    return jnp.concatenate([real_out, imag_out], -1)


def adjoint(blocks, vector):
    half = blocks.shape[-2]
    wide = blocks.astype(jnp.float32)
    from_real = jnp.sum(wide * vector[..., :half, None], -2)
    from_imag = jnp.sum(wide * vector[..., half:, None], -2)
    return jnp.concatenate(
        [
            from_real[..., :half] + from_imag[..., half:],
            from_imag[..., :half] - from_real[..., half:],
        ],
        -1,
    )


def turned_blocks(blocks):
    half = blocks.shape[-2]
    real, imag = blocks[..., :half], blocks[..., half:]
    return jnp.concatenate([real, -imag], -1), jnp.concatenate([imag, real], -1)


def adjoint_turned(pair, hop, vector):
    real_blocks, imag_blocks = (part[:, :, hop].astype(jnp.float32) for part in pair)
    half = real_blocks.shape[-2]
    terms = real_blocks * vector[..., :half, None] + imag_blocks * vector[..., half:, None]
    return jnp.sum(terms, -2)


def apply_operator(field, self_block, hop_blocks, pair):
    signs = chirality_signs(field.shape[-1])
    flipped = field * signs
    if pair is None:
        carried = lambda hop: adjoint(hop_blocks[:, :, hop], flipped)
    else:
        carried = lambda hop: adjoint_turned(pair, hop, flipped)
    carried_t = carried(3)
    ahead_t, behind_t = exchanged(field, carried_t, T_AXES)
    ahead_z = shifted(field, Z_AXES, -1)
    carried_z = carried(2)
    behind_z = shifted(carried_z, Z_AXES, 1)
    if pair is None:
        pair = lax.optimization_barrier(turned_blocks(hop_blocks))
    near = forward_sum(self_block[:, :, None], field[:, :, None])
    near_hops = jnp.stack([jnp.roll(field, -1, 1), jnp.roll(field, -1, 0)], 2)
    near = near + forward_sum(hop_blocks[:, :, :2], near_hops)
    near_back = jnp.roll(carried(0), 1, 1) + jnp.roll(carried(1), 1, 0)
    near = near + signs * near_back
    far = forward_sum(hop_blocks[:, :, 2:], jnp.stack([ahead_z, ahead_t], 2))
    return near + far + signs * (behind_z + behind_t), pair


def gram_body(v0, v1, v2, v3, out):
    vectors = [v0[...], v1[...], v2[...], v3[...]]
    half = vectors[0].shape[-1] // 2
    lane = lax.broadcasted_iota(jnp.int32, vectors[0].shape, 1)
    sign = jnp.where(lane < half, 1.0, -1.0)
    turned = [pltpu.roll(v, half, 1) * sign for v in vectors]
    rows = [jnp.sum(vectors[i] * vectors[i], 0, keepdims=True) for i in DIAGONAL]
    for i, j in PAIRS:
        rows.append(jnp.sum(vectors[i] * vectors[j], 0, keepdims=True))
        rows.append(jnp.sum(vectors[i] * turned[j], 0, keepdims=True))
    rows.append(jnp.zeros_like(rows[0]))
    stacked = jnp.concatenate(rows, 0)
    totals = jnp.sum(stacked, 1, keepdims=True)
    row = lax.broadcasted_iota(jnp.int32, stacked.shape, 0)
    column = lax.broadcasted_iota(jnp.int32, stacked.shape, 1)
    packed = jnp.sum(jnp.where(row == column, totals, 0.0), 0, keepdims=True)
    out[...] = jnp.broadcast_to(packed[None], out.shape)


def cmul(a, b):
    return (a[0] * b[0] - a[1] * b[1], a[0] * b[1] + a[1] * b[0])


def cmulc(a, b):
    return (a[0] * b[0] + a[1] * b[1], a[0] * b[1] - a[1] * b[0])


def cadd(a, b):
    return (a[0] + b[0], a[1] + b[1])


def csub(a, b):
    return (a[0] - b[0], a[1] - b[1])


def gram_image(gram, vec):
    image = {}
    for i in range(4):
        total = None
        for j, value in vec.items():
            if (i, j) not in gram:
                continue
            term = cmul(gram[i, j], value)
            total = term if total is None else cadd(total, term)
        image[i] = total
    return image


def inner(left, image):
    total = None
    for i, value in left.items():
        term = cmulc(value, image[i])
        total = term if total is None else cadd(total, term)
    return total


def combine(base, scale, vec):
    out = dict(base)
    for i, value in vec.items():
        term = cmul(scale, value)
        out[i] = csub(out[i], term) if i in out else (-term[0], -term[1])
    return out


def cycle_coefficients(gram, one):
    zero = jnp.zeros_like(one)
    residual = {0: (one, zero)}
    answer = {}
    basis_list = []
    direction_list = []
    for _ in range(ITERS):
        mapped = {i + 1: value for i, value in residual.items()}
        image = gram_image(gram, mapped)
        norm = inner(mapped, image)[0]
        along = inner(residual, image)
        along = (along[0], -along[1])
        orthogonal = mapped
        direction = residual
        squared = norm
        for basis, previous in zip(basis_list, direction_list):
            proj = inner(basis, image)
            squared = squared - (proj[0] * proj[0] + proj[1] * proj[1])
            orthogonal = combine(orthogonal, proj, basis)
            direction = combine(direction, proj, previous)
        scale = 1.0 / jnp.sqrt(squared)
        new_basis = {i: (v[0] * scale, v[1] * scale) for i, v in orthogonal.items()}
        new_direction = {i: (v[0] * scale, v[1] * scale) for i, v in direction.items()}
        step = (along[0] * scale, along[1] * scale)
        minus = (-step[0], -step[1])
        answer = combine(answer, minus, new_direction)
        residual = combine(residual, step, new_basis)
        basis_list.append(new_basis)
        direction_list.append(new_direction)
    return answer, residual


def gram_of(totals):
    gram = {}
    for k, i in enumerate(DIAGONAL):
        gram[i, i] = (totals[k], jnp.zeros_like(totals[k]))
    for k, (i, j) in enumerate(PAIRS):
        real, imag = totals[3 + 2 * k], totals[4 + 2 * k]
        gram[i, j] = (real, imag)
        gram[j, i] = (real, -imag)
    return gram


def finish_body(gathered, v0, v1, v2, v3, answer_out, residual_out):
    vectors = [v0[...], v1[...], v2[...], v3[...]]
    half = vectors[0].shape[-1] // 2
    spread = jnp.broadcast_to(jnp.sum(gathered[...], 0), (16, 2 * half))
    row = lax.broadcasted_iota(jnp.int32, spread.shape, 0)
    column = lax.broadcasted_iota(jnp.int32, spread.shape, 1)
    totals = jnp.sum(jnp.where(row == column, spread, 0.0), 1, keepdims=True)
    entries = [totals[k : k + 1, :] for k in range(15)]
    answer, residual = cycle_coefficients(gram_of(entries), jnp.ones_like(entries[0]))
    lane = lax.broadcasted_iota(jnp.int32, vectors[0].shape, 1)
    sign = jnp.where(lane < half, -1.0, 1.0)
    turned = [pltpu.roll(v, half, 1) * sign for v in vectors]
    for coefficients, out in ((answer, answer_out), (residual, residual_out)):
        total = None
        for i, (real, imag) in coefficients.items():
            term = real * vectors[i] + imag * turned[i]
            total = term if total is None else total + term
        out[...] = total


def on_chip(array):
    return pltpu.with_memory_space_constraint(array, pltpu.VMEM)


def on_device(right_side, self_block, hop_blocks):
    shape = right_side.shape
    sites = shape[2:]
    rows = (sites[0] * sites[1], sites[2])
    local_self = self_block[0, 0]
    local_hops = hop_blocks[0, 0]
    vectors = [lax.optimization_barrier(right_side[0, 0].astype(jnp.float32))]
    pair = None
    for _ in range(ITERS):
        field, pair = apply_operator(vectors[-1], local_self, local_hops, pair)
        vectors.append(field)
    flat = [on_chip(v.reshape(rows)) for v in vectors]
    space = pl.BlockSpec(memory_space=pltpu.VMEM)
    near_axes, far_axes = ("tx", "sy", "sc"), "tz"
    copies = pl.pallas_call(
        gram_body,
        out_shape=pltpu.VMEM((lax.axis_size(near_axes), 1, rows[1]), jnp.float32),
        in_specs=[space] * 4,
        out_specs=space,
    )(*flat)
    gathered = lax.all_to_all(copies, near_axes, 0, 0, tiled=True)
    packed = jnp.sum(gathered, 0, keepdims=True)
    copies = jnp.broadcast_to(packed, (lax.axis_size(far_axes), 1, rows[1]))
    gathered = lax.all_to_all(copies, far_axes, 0, 0, tiled=True)
    result = jax.ShapeDtypeStruct(rows, jnp.float32)
    answer, residual = pl.pallas_call(
        finish_body,
        out_shape=(result, result),
        in_specs=[space] * 5,
        out_specs=(space, space),
    )(on_chip(gathered), *flat)
    return answer.reshape(shape), residual.reshape(shape)


def solution(mesh):
    chips = mesh.devices.reshape(16, 4, 8, 2)
    fine = Mesh(chips, (*T_AXES, *Z_AXES))
    lead = (T_AXES, Z_AXES)
    placed = (P(*lead), P(*lead), P(*lead))
    return jax.shard_map(
        on_device,
        mesh=fine,
        in_specs=placed,
        out_specs=(P(*lead), P(*lead)),
        check_vma=False,
    )
```

```python
import jax
import jax.numpy as jnp
from jax import lax
from jax.experimental import pallas as pl
from jax.experimental.pallas import tpu as pltpu
from jax.sharding import Mesh
from jax.sharding import PartitionSpec as P


ITERS = 3
T_AXES = ("tz", "tx")
Z_AXES = ("sy", "sc")
DIAGONAL = (1, 2, 3)
PAIRS = ((0, 1), (0, 2), (0, 3), (1, 2), (1, 3), (2, 3))


def shifted(block, axes, distance):
    count = lax.axis_size(axes)
    route = [((i - distance) % count, i) for i in range(count)]
    return lax.ppermute(block, axes, route)


def exchanged(field, carried, axes):
    count = lax.axis_size(axes)
    even = lax.axis_index(axes) % 2 == 0
    across = lax.ppermute(
        jnp.where(even, field, carried),
        axes,
        [(i, (i + (1 if i % 2 else -1)) % count) for i in range(count)],
    )
    inside = lax.ppermute(jnp.where(even, carried, field), axes, [(i, i ^ 1) for i in range(count)])
    return jnp.where(even, inside, across), jnp.where(even, across, inside)


def chirality_signs(full_width):
    half_width = full_width // 2
    column = jnp.arange(full_width) % half_width
    return jnp.where(column < half_width // 2, 1.0, -1.0).astype(jnp.float32)


def forward_sum(blocks, vectors):
    half = blocks.shape[-2]
    plain = jnp.concatenate([vectors[..., :half], -vectors[..., half:]], -1)
    turned = jnp.concatenate([vectors[..., half:], vectors[..., :half]], -1)
    wide = blocks.astype(jnp.float32)
    real_out = jnp.sum(wide * plain[..., None, :], (-3, -1))
    imag_out = jnp.sum(wide * turned[..., None, :], (-3, -1))
    return jnp.concatenate([real_out, imag_out], -1)


def on_chip(array):
    return pltpu.with_memory_space_constraint(array, pltpu.VMEM)


def turned_blocks(blocks):
    half = blocks.shape[-2]
    real, imag = blocks[..., :half], blocks[..., half:]
    return jnp.concatenate([real, -imag], -1), jnp.concatenate([imag, real], -1)


def adjoint_turned(pair, hop, vector):
    real_blocks, imag_blocks = (part[:, :, hop].astype(jnp.float32) for part in pair)
    half = real_blocks.shape[-2]
    terms = real_blocks * vector[..., :half, None] + imag_blocks * vector[..., half:, None]
    return jnp.sum(terms, -2)


def forward_turned(pair, hops, vectors):
    outs = [
        jnp.sum(part[:, :, hops].astype(jnp.float32) * vectors[..., None, :], (2, 4))
        for part in pair
    ]
    return jnp.concatenate(outs, -1)


def first_carry_body(right_side, blocks, vector, carried_z, carried_t):
    rows = right_side[...].astype(jnp.float32)
    vector[...] = rows
    half = rows.shape[-1] // 2
    column = lax.broadcasted_iota(jnp.int32, (1, half), 1)
    flips = jnp.where(column < half // 2, 1.0, -1.0)
    lane = lax.broadcasted_iota(jnp.int32, (1, 2 * half), 1)
    sign = jnp.where(lane < half, 1.0, -1.0)
    for site in range(rows.shape[0]):
        row = rows[site : site + 1]
        parts = jnp.concatenate([row[:, :half] * flips, row[:, half:] * flips], 0)
        parts = parts.astype(jnp.bfloat16)
        for hop, out in enumerate((carried_z, carried_t)):
            product = jnp.dot(parts, blocks[site, hop], preferred_element_type=jnp.float32)
            turned = pltpu.roll(product, half, 1)
            out[site : site + 1, :] = turned[1:2] + sign * product[0:1]


def first_carry(right_side, blocks):
    sites = right_side.shape[0] * right_side.shape[1]
    width = right_side.shape[-1]
    result = pltpu.VMEM((sites, width), jnp.float32)
    row_spec = pl.BlockSpec((sites, width), lambda i: (0, 0))
    outs = pl.pallas_call(
        first_carry_body,
        grid=(1,),
        out_shape=(result,) * 3,
        in_specs=[
            row_spec,
            pl.BlockSpec((sites, 2, *blocks.shape[3:]), lambda i: (0, 1, 0, 0)),
        ],
        out_specs=(row_spec,) * 3,
    )(right_side.reshape(sites, width), blocks.reshape(sites, *blocks.shape[2:]))
    return [out.reshape(right_side.shape) for out in outs]


def apply_operator(field, self_block, hop_blocks, pair, carried_z, carried_t):
    signs = chirality_signs(field.shape[-1])
    flipped = field * signs
    if carried_t is None:
        carried_t = adjoint_turned(pair, 3, flipped)
    ahead_t, behind_t = exchanged(field, carried_t, T_AXES)
    ahead_z = shifted(field, Z_AXES, -1)
    if carried_z is None:
        carried_z = adjoint_turned(pair, 2, flipped)
    behind_z = shifted(carried_z, Z_AXES, 1)
    if pair is None:
        pair = lax.optimization_barrier(turned_blocks(hop_blocks))
    near = forward_sum(self_block[:, :, None], field[:, :, None])
    near_hops = jnp.stack([jnp.roll(field, -1, 1), jnp.roll(field, -1, 0)], 2)
    near = near + forward_turned(pair, slice(0, 2), near_hops)
    carried_x, carried_y = (adjoint_turned(pair, hop, flipped) for hop in (0, 1))
    near = near + signs * (jnp.roll(carried_x, 1, 1) + jnp.roll(carried_y, 1, 0))
    near = near + forward_turned(pair, slice(2, 3), ahead_z[:, :, None]) + signs * behind_z
    far = forward_turned(pair, slice(3, 4), ahead_t[:, :, None])
    return near + far + signs * behind_t, pair


def gram_body(v0, v1, v2, v3, out):
    vectors = [v0[...], v1[...], v2[...], v3[...]]
    half = vectors[0].shape[-1] // 2
    lane = lax.broadcasted_iota(jnp.int32, vectors[0].shape, 1)
    sign = jnp.where(lane < half, 1.0, -1.0)
    turned = [pltpu.roll(v, half, 1) * sign for v in vectors]
    rows = [jnp.sum(vectors[i] * vectors[i], 0, keepdims=True) for i in DIAGONAL]
    for i, j in PAIRS:
        rows.append(jnp.sum(vectors[i] * vectors[j], 0, keepdims=True))
        rows.append(jnp.sum(vectors[i] * turned[j], 0, keepdims=True))
    rows.append(jnp.zeros_like(rows[0]))
    stacked = jnp.concatenate(rows, 0)
    totals = jnp.sum(stacked, 1, keepdims=True)
    row = lax.broadcasted_iota(jnp.int32, stacked.shape, 0)
    column = lax.broadcasted_iota(jnp.int32, stacked.shape, 1)
    packed = jnp.sum(jnp.where(row == column, totals, 0.0), 0, keepdims=True)
    out[...] = jnp.broadcast_to(packed[None], out.shape)


def cmul(a, b):
    return (a[0] * b[0] - a[1] * b[1], a[0] * b[1] + a[1] * b[0])


def cmulc(a, b):
    return (a[0] * b[0] + a[1] * b[1], a[0] * b[1] - a[1] * b[0])


def cadd(a, b):
    return (a[0] + b[0], a[1] + b[1])


def csub(a, b):
    return (a[0] - b[0], a[1] - b[1])


def gram_image(gram, vec):
    image = {}
    for i in range(4):
        total = None
        for j, value in vec.items():
            if (i, j) not in gram:
                continue
            term = cmul(gram[i, j], value)
            total = term if total is None else cadd(total, term)
        image[i] = total
    return image


def inner(left, image):
    total = None
    for i, value in left.items():
        term = cmulc(value, image[i])
        total = term if total is None else cadd(total, term)
    return total


def combine(base, scale, vec):
    out = dict(base)
    for i, value in vec.items():
        term = cmul(scale, value)
        out[i] = csub(out[i], term) if i in out else (-term[0], -term[1])
    return out


def cycle_coefficients(gram, one):
    zero = jnp.zeros_like(one)
    residual = {0: (one, zero)}
    answer = {}
    basis_list = []
    direction_list = []
    for _ in range(ITERS):
        mapped = {i + 1: value for i, value in residual.items()}
        image = gram_image(gram, mapped)
        norm = inner(mapped, image)[0]
        along = inner(residual, image)
        along = (along[0], -along[1])
        orthogonal = mapped
        direction = residual
        squared = norm
        for basis, previous in zip(basis_list, direction_list):
            proj = inner(basis, image)
            squared = squared - (proj[0] * proj[0] + proj[1] * proj[1])
            orthogonal = combine(orthogonal, proj, basis)
            direction = combine(direction, proj, previous)
        scale = 1.0 / jnp.sqrt(squared)
        new_basis = {i: (v[0] * scale, v[1] * scale) for i, v in orthogonal.items()}
        new_direction = {i: (v[0] * scale, v[1] * scale) for i, v in direction.items()}
        step = (along[0] * scale, along[1] * scale)
        minus = (-step[0], -step[1])
        answer = combine(answer, minus, new_direction)
        residual = combine(residual, step, new_basis)
        basis_list.append(new_basis)
        direction_list.append(new_direction)
    return answer, residual


def gram_of(totals):
    gram = {}
    for k, i in enumerate(DIAGONAL):
        gram[i, i] = (totals[k], jnp.zeros_like(totals[k]))
    for k, (i, j) in enumerate(PAIRS):
        real, imag = totals[3 + 2 * k], totals[4 + 2 * k]
        gram[i, j] = (real, imag)
        gram[j, i] = (real, -imag)
    return gram


def finish_body(gathered, v0, v1, v2, v3, answer_out, residual_out):
    vectors = [v0[...], v1[...], v2[...], v3[...]]
    half = vectors[0].shape[-1] // 2
    spread = jnp.broadcast_to(jnp.sum(gathered[...], 0), (16, 2 * half))
    row = lax.broadcasted_iota(jnp.int32, spread.shape, 0)
    column = lax.broadcasted_iota(jnp.int32, spread.shape, 1)
    totals = jnp.sum(jnp.where(row == column, spread, 0.0), 1, keepdims=True)
    entries = [totals[k : k + 1, :] for k in range(15)]
    answer, residual = cycle_coefficients(gram_of(entries), jnp.ones_like(entries[0]))
    lane = lax.broadcasted_iota(jnp.int32, vectors[0].shape, 1)
    sign = jnp.where(lane < half, -1.0, 1.0)
    turned = [pltpu.roll(v, half, 1) * sign for v in vectors]
    for coefficients, out in ((answer, answer_out), (residual, residual_out)):
        total = None
        for i, (real, imag) in coefficients.items():
            term = real * vectors[i] + imag * turned[i]
            total = term if total is None else total + term
        out[...] = total


def on_device(right_side, self_block, hop_blocks):
    shape = right_side.shape
    sites = shape[2:]
    rows = (sites[0] * sites[1], sites[2])
    local_self = self_block[0, 0]
    local_hops = hop_blocks[0, 0]
    first, *carried = first_carry(right_side[0, 0], local_hops)
    vectors = [first]
    pair = None
    for _ in range(ITERS):
        field, pair = apply_operator(vectors[-1], local_self, local_hops, pair, *carried)
        vectors.append(field)
        carried = [None, None]
    flat = [on_chip(v.reshape(rows)) for v in vectors]
    space = pl.BlockSpec(memory_space=pltpu.VMEM)
    near_axes, far_axes = "tz", ("tx", "sy", "sc")
    copies = pl.pallas_call(
        gram_body,
        out_shape=pltpu.VMEM((lax.axis_size(near_axes), 1, rows[1]), jnp.float32),
        in_specs=[space] * 4,
        out_specs=space,
    )(*flat)
    gathered = lax.all_to_all(copies, near_axes, 0, 0, tiled=True)
    packed = jnp.sum(gathered, 0, keepdims=True)
    copies = jnp.broadcast_to(packed, (lax.axis_size(far_axes), 1, rows[1]))
    gathered = lax.all_to_all(copies, far_axes, 0, 0, tiled=True)
    result = jax.ShapeDtypeStruct(rows, jnp.float32)
    answer, residual = pl.pallas_call(
        finish_body,
        out_shape=(result, result),
        in_specs=[space] * 5,
        out_specs=(space, space),
    )(on_chip(gathered), *flat)
    return answer.reshape(shape), residual.reshape(shape)


def solution(mesh):
    chips = mesh.devices.reshape(16, 4, 8, 2)
    fine = Mesh(chips, (*T_AXES, *Z_AXES))
    lead = (T_AXES, Z_AXES)
    placed = (P(*lead), P(*lead), P(*lead))
    return jax.shard_map(
        on_device,
        mesh=fine,
        in_specs=placed,
        out_specs=(P(*lead), P(*lead)),
        check_vma=False,
    )
```
